32 devices in a mesh: ctx: 8 (over z, y), tp: 4 (over x, core).
Axes of the slice: x: 2, y: 2, z: 4, core: 2. Of those that a mesh axis runs over, the one named last changes fastest.
Arguments:
- queries: bfloat16 [1024, 8192], P('ctx', 'tp'), may hold values from -6 to 6
- keys: bfloat16 [1024, 8192], P('ctx', 'tp'), may hold values from -6 to 6
- values: bfloat16 [1024, 8192], P('ctx', 'tp'), may hold values from -6 to 6
- short_taps: float32 [3, 3, 8192], P(None, None, 'tp'), may hold values from -3.5 to 3.5
- long_rates: float32 [8192, 16], P('tp'), may hold values from 1.953125e-05 to 0.05
- long_resid: float32 [8192, 16], P('tp'), may hold values from -1.5 to 1.5
- out_weight: bfloat16 [8192, 4096], P('tp'), may hold values from -0.09375 to 0.09375
Outputs:
- block_out: bfloat16 [1024, 4096], P('ctx', 'tp')
The draws below stay inside these ranges and needn't reach their ends.
All inputs are finite; a program needn't handle non-finite values.
Results may differ from the reference program's by a relative error of at most 0.017.
Values may be sent and summed in bfloat16 or wider, within the bound.
No kernel may reach another device: no remote copies, remote signals or barrier semaphores. Data moves between devices by JAX's collectives and lax.ppermute only.
A program may use at most 128 MiB of HBM per device.

```python
import math
import jax
import jax.numpy as jnp
from jax import lax

D = 8192
OUT = 4096
MODES = 16
SHORT = 3
SEQ = 1024


def raised(array, stream_key, source, target, parts, factor):
    owner, partner = [(jnp.arange(array.shape[position]) // (array.shape[position] // parts)).reshape([-1 if axis == position else 1 for axis in range(array.ndim)]) for position in (source, target)]
    chosen = jax.random.permutation(stream_key, parts)[partner]
    strong = (owner == chosen) | (owner == (partner + parts // 2) % parts)
    return jnp.where(strong, factor * array, array)


def steps_of(key, extent, split, least, top_value):
    loudness, own = 1.0, jax.random.fold_in(key, 6)
    for position, shards_of in split:
        steps = jnp.exp(jax.random.uniform(jax.random.fold_in(own, position), (shards_of,), jnp.float32, least / len(split), top_value / len(split)))
        loudness = loudness * jnp.repeat(steps, extent[position] // shards_of).reshape([-1 if axis == position else 1 for axis in range(len(extent))])
    return loudness


def scatter_about(rng, dims, scale, limit, split=(), kind=jnp.bfloat16):
    drawn = scale * jax.random.normal(rng, dims, jnp.float32)
    if split:
        drawn = drawn * steps_of(rng, dims, split, -0.22, 0.18)
    return jnp.clip(drawn, -limit, limit).astype(kind)


def noise_with(stream_key, shape, scale, bound, pieces, heavy, held_as=jnp.bfloat16):
    drawn = scale * jax.random.normal(stream_key, shape, jnp.float32)
    if pieces:
        drawn = drawn * steps_of(stream_key, shape, pieces, -0.22, 0.18)
    return jnp.clip(raised(drawn, jax.random.fold_in(stream_key, 3), *heavy), -bound, bound).astype(held_as)


def setup_inputs(seed: int = 0) -> dict:
    arg_keys = jax.random.split(jax.random.key(seed), 8)
    queries = scatter_about(arg_keys[0], (SEQ, D), 1.0, 6.0, ((0, 8), (1, 4)))
    keys = scatter_about(arg_keys[1], (SEQ, D), 1.0, 6.0, ((0, 8), (1, 4)))
    values = scatter_about(arg_keys[2], (SEQ, D), 1.0, 6.0, ((0, 8), (1, 4)))
    short_taps = scatter_about(arg_keys[3], (3, SHORT, D), SHORT ** -0.5, 3.5, ((2, 4),), jnp.float32)
    long_rates = jnp.clip(jnp.exp(math.log(0.05) - 7.8477626 * jax.random.uniform(arg_keys[4], (D, MODES), jnp.float32) ** steps_of(arg_keys[4], (D, MODES), ((0, 4),), -0.2, 0.2)), 1.9531249563442543e-05, 0.05)
    long_resid = scatter_about(arg_keys[5], (D, MODES), 0.25, 1.5, ((0, 4),), jnp.float32)
    out_weight = noise_with(arg_keys[6], (D, OUT), D ** -0.5, 0.09375, ((0, 4),), (0, 1, 4, 2.0))
    return {"queries": queries, "keys": keys, "values": values, "short_taps": short_taps, "long_rates": long_rates, "long_resid": long_resid, "out_weight": out_weight}


def short_filter(stream, filter_taps):
    tail_len = filter_taps.shape[0] - 1
    length = stream.shape[0]
    leading = jnp.zeros((tail_len, stream.shape[1]), stream.dtype)
    extended = jnp.concatenate([leading, stream], axis=0).astype(jnp.float32)
    accum_sum = jnp.zeros(stream.shape, jnp.float32)
    for tap_index in range(filter_taps.shape[0]):
        accum_sum = accum_sum + filter_taps[tap_index] * extended[tail_len - tap_index:tail_len - tap_index + length]
    return accum_sum

def long_filter(product, long_rates, long_resid):
    decay = jnp.exp(-long_rates)
    coeff = long_resid * jnp.sqrt(-jnp.expm1(-2.0 * long_rates))

    def advance(carry_state, row_in):
        carry_state = decay * carry_state + row_in.astype(jnp.float32)[:, None]
        return (carry_state, lax.optimization_barrier(jnp.sum(coeff * carry_state, axis=1)))
    start_state = jnp.zeros(long_rates.shape, jnp.float32)
    _, result = lax.scan(advance, start_state, product)
    return result

def reference(queries, keys, values, short_taps, long_rates, long_resid, out_weight):
    q_feat = short_filter(queries, short_taps[0])
    k_feat = short_filter(keys, short_taps[1])
    v_feat = short_filter(values, short_taps[2])
    product = (k_feat * v_feat).astype(jnp.bfloat16)
    long_out = long_filter(product, long_rates, long_resid).astype(jnp.bfloat16)
    long_out = lax.optimization_barrier(long_out)
    gated = (q_feat * long_out.astype(jnp.float32)).astype(jnp.bfloat16)
    return jnp.dot(gated, out_weight, preferred_element_type=jnp.float32).astype(jnp.bfloat16)
```

```python
import functools

import jax
import jax.numpy as jnp
from jax import lax
from jax.experimental import pallas as pl
from jax.experimental.pallas import tpu as pltpu
from jax.sharding import PartitionSpec as P

LANES = 128
VMEM = pltpu.VMEM


def whole():
    return pl.BlockSpec(memory_space=VMEM)


def to_rows(source, target, first, groups):
    count = source.shape[0]
    for group in range(groups):
        piece = source[:, group * LANES : (group + 1) * LANES].astype(jnp.float32)
        target[pl.ds(first * groups + group, count, stride=groups), :] = piece


def spread(stream_ref, halo, target, groups):
    tail = halo.shape[0]
    to_rows(halo, target, 0, groups)
    step = 16

    def body(index, carry):
        start = pl.multiple_of(index * step, step)
        for group in range(groups):
            piece = stream_ref[pl.ds(start, step), group * LANES : (group + 1) * LANES]
            row = (start + tail) * groups + group
            target[pl.ds(row, step, stride=groups), :] = piece.astype(jnp.float32)
        return carry

    lax.fori_loop(0, stream_ref.shape[0] // step, body, 0)


def row_block(index, groups, offset, height):
    start = index * groups + offset
    return pl.ds(pl.multiple_of(start, height), height)


def chunks(groups):
    height = min(8, groups)
    return height, range(0, groups, height)


def state_kernel(tail, groups, halo_ref, k_ref, v_ref, taps_ref, rates_ref, x_ref, state_ref, rate_ref, k_rows, v_rows, tap_rows):
    tokens = k_ref.shape[0]
    modes = rates_ref.shape[0]
    halo = halo_ref[...].astype(jnp.float32)
    spread(k_ref, halo[0:tail], k_rows, groups)
    spread(v_ref, halo[tail : 2 * tail], v_rows, groups)
    to_rows(rates_ref[...], rate_ref, 0, groups)
    taps = tail + 1
    for which in range(2):
        to_rows(taps_ref[1 + which], tap_rows, which * taps, groups)
    height, offsets = chunks(groups)
    for offset in offsets:
        decay = [jnp.exp(-rate_ref[row_block(m, groups, offset, height), :]) for m in range(modes)]
        tap = [tap_rows[row_block(j, groups, offset, height), :] for j in range(2 * taps)]

        def body(position, carry, decay=decay, tap=tap, offset=offset):
            k_old, v_old, state = carry
            k_all = k_old + [k_rows[row_block(position + tail, groups, offset, height), :]]
            v_all = v_old + [v_rows[row_block(position + tail, groups, offset, height), :]]
            k_feat = tap[0] * k_all[tail]
            v_feat = tap[taps] * v_all[tail]
            for j in range(1, taps):
                k_feat = k_feat + tap[j] * k_all[tail - j]
                v_feat = v_feat + tap[taps + j] * v_all[tail - j]
            product = (k_feat * v_feat).astype(jnp.bfloat16).astype(jnp.float32)
            x_ref[row_block(position, groups, offset, height), :] = product
            state = [d * s + product for d, s in zip(decay, state)]
            return k_all[1:], v_all[1:], state

        lead = lambda rows: [rows[row_block(j, groups, offset, height), :] for j in range(tail)]
        zero = [jnp.zeros((height, LANES), jnp.float32)] * modes
        _, _, state = lax.fori_loop(0, tokens, body, (lead(k_rows), lead(v_rows), zero), unroll=4)
        for m in range(modes):
            state_ref[row_block(m, groups, offset, height), :] = state[m]


def local_kernel(tail, groups, halo_ref, q_ref, taps_ref, x_ref, rate_ref, gains_ref, y_ref, qf_ref, gain_ref, q_rows, tap_rows):
    tokens = q_ref.shape[0]
    modes = gains_ref.shape[0]
    taps = tail + 1
    halo = halo_ref[...].astype(jnp.float32)
    spread(q_ref, halo[2 * tail : 3 * tail], q_rows, groups)
    to_rows(gains_ref[...], gain_ref, 0, groups)
    to_rows(taps_ref[0], tap_rows, 0, groups)
    height, offsets = chunks(groups)
    for offset in offsets:
        block = lambda ref, row, offset=offset: ref[row_block(row, groups, offset, height), :]
        tap = [block(tap_rows, j) for j in range(taps)]

        def gate(position, old, tap=tap, offset=offset, block=block):
            rows = old + [block(q_rows, position + tail)]
            feat = tap[0] * rows[tail]
            for j in range(1, taps):
                feat = feat + tap[j] * rows[tail - j]
            qf_ref[row_block(position, groups, offset, height), :] = feat
            return rows[1:]

        lax.fori_loop(0, tokens, gate, [block(q_rows, j) for j in range(tail)], unroll=8)
        decay = [jnp.exp(-block(rate_ref, m)) for m in range(modes)]
        gain = [block(gain_ref, m) for m in range(modes)]

        def body(position, state, decay=decay, gain=gain, offset=offset, block=block):
            product = block(x_ref, position)
            state = [d * s + product for d, s in zip(decay, state)]
            terms = [c * s for c, s in zip(gain, state)]
            while len(terms) > 1:
                terms = [a + b for a, b in zip(terms[::2], terms[1::2])]
            y_ref[row_block(position, groups, offset, height), :] = terms[0]
            return state

        zero = [jnp.zeros((height, LANES), jnp.float32)] * modes
        lax.fori_loop(0, tokens, body, zero, unroll=4)


def carry_kernel(groups, carry_ref, rate_ref, gain_ref, y_ref, qf_ref, gated_ref, rows):
    tokens = gated_ref.shape[0]
    modes = carry_ref.shape[0] // groups
    height, offsets = chunks(groups)
    for offset in offsets:
        block = lambda ref, row, offset=offset: ref[row_block(row, groups, offset, height), :]
        decay = [jnp.exp(-block(rate_ref, m)) for m in range(modes)]
        start = [block(gain_ref, m) * block(carry_ref, m) for m in range(modes)]

        def body(position, state, decay=decay, offset=offset, block=block):
            state = [d * s for d, s in zip(decay, state)]
            terms = list(state)
            while len(terms) > 1:
                terms = [a + b for a, b in zip(terms[::2], terms[1::2])]
            total = block(y_ref, position) + terms[0]
            rounded = total.astype(jnp.bfloat16).astype(jnp.float32)
            rows[row_block(position, groups, offset, height), :] = block(qf_ref, position) * rounded
            return state

        lax.fori_loop(0, tokens, body, start, unroll=4)
    step = 16

    def gather(index, carry):
        begin = pl.multiple_of(index * step, step)
        for group in range(groups):
            piece = rows[pl.ds(begin * groups + group, step, stride=groups), :]
            gated_ref[pl.ds(begin, step), group * LANES : (group + 1) * LANES] = piece.astype(jnp.bfloat16)
        return carry

    lax.fori_loop(0, tokens // step, gather, 0)


def matmul_kernel(which_ref, gated_ref, weight_ref, out_ref):
    del which_ref
    out_ref[...] = jnp.dot(
        gated_ref[...], weight_ref[...], preferred_element_type=jnp.float32
    ).astype(out_ref.dtype)


def project(gated, weight, which, columns, kind):
    tokens, channels = gated.shape
    tile = min(columns, 256)
    steps = columns // tile
    spec = pltpu.PrefetchScalarGridSpec(
        num_scalar_prefetch=1,
        grid=(steps,),
        in_specs=[
            pl.BlockSpec((tokens, channels), lambda i, w: (0, 0)),
            pl.BlockSpec((channels, tile), lambda i, w: (0, w[0] * steps + i)),
        ],
        out_specs=pl.BlockSpec((tokens, tile), lambda i, w: (0, i)),
    )
    return pl.pallas_call(
        matmul_kernel,
        grid_spec=spec,
        out_shape=jax.ShapeDtypeStruct((tokens, columns), kind),
        cost_estimate=pl.CostEstimate(
            flops=2 * tokens * channels * columns,
            bytes_accessed=2 * channels * columns,
            transcendentals=0,
        ),
    )(which.reshape(1), gated, weight)


def swap(value, axis, bits):
    count = lax.axis_size(axis)
    return lax.ppermute(value, axis, [(i, i ^ bits) for i in range(count)])


def radices(count):
    found = []
    while count > 1:
        radix = 2 if not found or count == 2 else 4
        found.append(radix)
        count //= radix
    return found


def carried(state, rate, tokens):
    count = lax.axis_size("ctx")
    index = lax.axis_index("ctx")
    total, before, stride = state, None, 1
    per_device = rate * float(tokens)

    def weight(steps):
        return jnp.exp(-per_device * steps.astype(jnp.float32))

    rounds = radices(count)
    for radix in rounds:
        sent = total.astype(jnp.bfloat16)
        digit = (index // stride) % radix
        others = [(digit ^ j, swap(sent, "ctx", j * stride)) for j in reversed(range(1, radix))]
        inside = index % stride
        new = None
        summed = total * weight(stride * (radix - 1 - digit))
        for place, value in others:
            value = value.astype(jnp.float32)
            steps = jnp.maximum(stride * (digit - 1 - place), 0) + inside
            term = jnp.where(place < digit, weight(steps) * value, 0.0)
            new = term if new is None else new + term
            summed = summed + weight(stride * (radix - 1 - place)) * value
        before = new if before is None else before + new
        total = summed
        stride *= radix
    return jnp.zeros_like(state) if before is None else before


def shards(queries, keys, values, short_taps, long_rates, long_resid, out_weight):
    tokens, channels = queries.shape
    streams, taps, _ = short_taps.shape
    modes = long_rates.shape[1]
    tail = taps - 1
    groups = channels // LANES
    f32 = jnp.float32
    rows = lambda count: jax.ShapeDtypeStruct((count * groups, LANES), f32)
    scratch = lambda count: VMEM((count * groups, LANES), f32)
    ends = jnp.concatenate([item[tokens - tail :] for item in (keys, values, queries)], axis=0)
    count = lax.axis_size("ctx")
    halo = lax.ppermute(ends, "ctx", [(i, i + 1) for i in range(count - 1)])
    rates = long_rates.T
    gains = (long_resid * jnp.sqrt(-jnp.expm1(-2.0 * long_rates))).T
    product, state, rate = pl.pallas_call(
        functools.partial(state_kernel, tail, groups),
        in_specs=[whole()] * 5,
        out_specs=[whole()] * 3,
        out_shape=[rows(tokens), rows(modes), rows(modes)],
        scratch_shapes=[scratch(tokens + tail), scratch(tokens + tail), scratch(2 * taps)],
    )(halo, keys, values, short_taps, rates)
    local, gate, gain = pl.pallas_call(
        functools.partial(local_kernel, tail, groups),
        in_specs=[whole()] * 6,
        out_specs=[whole()] * 3,
        out_shape=[rows(tokens), rows(tokens), rows(modes)],
        scratch_shapes=[scratch(tokens + tail), scratch(taps)],
        cost_estimate=pl.CostEstimate(
            flops=4 * tokens * channels * modes, bytes_accessed=8 * tokens * channels, transcendentals=0
        ),
    )(halo, queries, short_taps, product, rate, gains)
    before = carried(state, rate, tokens)
    gated = pl.pallas_call(
        functools.partial(carry_kernel, groups),
        in_specs=[whole()] * 5,
        out_specs=whole(),
        out_shape=jax.ShapeDtypeStruct((tokens, channels), jnp.bfloat16),
        scratch_shapes=[scratch(tokens)],
    )(before, rate, gain, local, gate)

    parts = lax.axis_size("tp")
    me = lax.axis_index("tp")
    columns = out_weight.shape[1] // parts
    cores = 2 if parts % 2 == 0 else 1
    arrived = []
    own = None
    for chip in reversed(range(0, parts, cores)):
        block = functools.partial(project, gated, out_weight, columns=columns)
        if cores == 2:
            given = swap(block(which=me ^ (chip + 1), kind=jnp.bfloat16), "tp", 1)
            summed = block(which=me ^ chip, kind=f32) + given.astype(f32)
        else:
            summed = block(which=me ^ chip, kind=f32)
        if chip:
            arrived.append(swap(summed.astype(jnp.bfloat16), "tp", chip))
        else:
            own = summed
    for item in arrived:
        own = own + item.astype(f32)
    return own.astype(jnp.bfloat16)


def solution(mesh):
    return jax.shard_map(
        shards,
        mesh=mesh,
        in_specs=(
            P("ctx", "tp"),
            P("ctx", "tp"),
            P("ctx", "tp"),
            P(None, None, "tp"),
            P("tp", None),
            P("tp", None),
            P("tp", None),
        ),
        out_specs=P("ctx", "tp"),
        check_vma=False,
    )
```

```python
import functools

import jax
import jax.numpy as jnp
from jax import lax
from jax.experimental import pallas as pl
from jax.experimental.pallas import tpu as pltpu
from jax.sharding import PartitionSpec as P

LANES = 128
SUBLANES = 8
VMEM = pltpu.VMEM
SMALL = pltpu.CompilerParams(vmem_limit_bytes=8 * 2**20)
F32, BF16 = jnp.float32, jnp.bfloat16


def here():
    return pl.BlockSpec(memory_space=VMEM)


def far():
    return pl.BlockSpec(memory_space=pltpu.HBM)


def factor(count, most):
    return max(size for size in range(1, most + 1) if count % size == 0)


def at(row, height):
    return pl.ds(pl.multiple_of(row * height, height), height)


def to_rows(source, target, first, part, height):
    count = source.shape[0]
    for group in range(height):
        lane = (part * height + group) * LANES
        target[pl.ds(first * height + group, count, stride=height), :] = source[:, lane : lane + LANES].astype(F32)


def spread(stream_ref, target, first, part, height):
    step = 16

    def body(index, carry):
        start = pl.multiple_of(index * step, step)
        to_rows(stream_ref.at[pl.ds(start, step)], target, first + start, part, height)
        return carry

    lax.fori_loop(0, stream_ref.shape[0] // step, body, 0)


def summed(terms):
    terms = list(terms)
    while len(terms) > 1:
        pairs = [a + b for a, b in zip(terms[::2], terms[1::2])]
        terms = pairs + terms[2 * len(pairs) :]
    return terms[0]


def convolved(taps, rows):
    return summed(tap * row for tap, row in zip(taps, reversed(rows)))


def rounded(value):
    return value.astype(BF16).astype(F32)


def fetch_kernel(tail, *refs):
    count = (len(refs) - 2) // 2
    sources, (ends_ref, *targets), sems = refs[:count], refs[count:-1], refs[-1]
    copies = [pltpu.make_async_copy(s, t, sems.at[i]) for i, (s, t) in enumerate(zip(sources, targets))]
    for copy in copies:
        copy.start()
    for copy in copies:
        copy.wait()
    tokens = targets[0].shape[0]
    last = [ref[tokens - 16 :, :].astype(F32)[16 - tail :] for ref in targets[:3]]
    ends_ref[...] = jnp.concatenate(last, axis=0).astype(BF16)


def state_kernel(tail, height, k_ref, v_ref, taps_ref, rates_ref, weight_ref, x_ref, state_ref, rate_ref, tap_ref, piece_ref, k_rows, v_rows, sem):
    rows = piece_ref.shape[0]
    copy = pltpu.make_async_copy(weight_ref.at[pl.ds(0, rows)], piece_ref, sem)
    copy.start()
    tokens, channels = k_ref.shape
    modes = rates_ref.shape[0]
    taps = tail + 1
    for part in range(channels // (height * LANES)):
        spread(k_ref, k_rows, 0, part, height)
        spread(v_ref, v_rows, 0, part, height)
        to_rows(rates_ref[...], rate_ref, part * modes, part, height)
        for which in range(2):
            to_rows(taps_ref[1 + which], tap_ref, (2 * part + which) * taps, part, height)
        decay = [jnp.exp(-rate_ref[at(part * modes + m, height), :]) for m in range(modes)]
        tap = [tap_ref[at(2 * part * taps + j, height), :] for j in range(2 * taps)]

        def body(position, carry, decay=decay, tap=tap, part=part):
            k_old, v_old, state = carry
            k_all = k_old + [k_rows[at(position, height), :]]
            v_all = v_old + [v_rows[at(position, height), :]]
            product = rounded(convolved(tap[:taps], k_all) * convolved(tap[taps:], v_all))
            x_ref[at(part * tokens + position, height), :] = product
            return k_all[1:], v_all[1:], [d * s + product for d, s in zip(decay, state)]

        lead = lambda rows: [rows[at(j, height), :] for j in range(tail)]
        zero = [jnp.zeros((height, LANES), F32)] * modes
        first = (lead(k_rows), lead(v_rows), zero)
        state = lax.fori_loop(tail, tokens, body, first, unroll=factor(tokens - tail, 8))[2]
        for m in range(modes):
            state_ref[at(part * modes + m, height), :] = state[m]
    copy.wait()


def first_kernel(tail, height, halo_ref, k_ref, v_ref, tap_ref, rate_ref, part_state_ref, start_ref, state_ref, sent_ref, k_rows, v_rows):
    tokens, channels = k_ref.shape
    taps = tail + 1
    parts = channels // (height * LANES)
    modes = rate_ref.shape[0] // (height * parts)
    halo = halo_ref[...].astype(F32)
    for part in range(parts):
        for which, (ref, rows) in enumerate(((k_ref, k_rows), (v_ref, v_rows))):
            to_rows(halo[which * tail : (which + 1) * tail], rows, 0, part, height)
            to_rows(ref[0:16].astype(F32)[:tail], rows, tail, part, height)
        tap = [tap_ref[at(2 * part * taps + j, height), :] for j in range(2 * taps)]
        products = []
        for position in range(tail):
            near = lambda rows: [rows[at(position + j, height), :] for j in range(taps)]
            product = rounded(convolved(tap[:taps], near(k_rows)) * convolved(tap[taps:], near(v_rows)))
            start_ref[at(part * tail + position, height), :] = product
            products.append(product)
        for m in range(modes):
            here_ = at(part * modes + m, height)
            rate = rate_ref[here_, :]
            late = [jnp.exp(-rate * float(tokens - 1 - j)) * product for j, product in enumerate(products)]
            state_ref[here_, :] = part_state_ref[here_, :] + summed(late)
    sent_ref[...] = state_ref[...].astype(BF16)


def gain_of(rate, resid):
    twice = 2.0 * rate
    series = jnp.ones_like(twice)
    for order in range(9, 1, -1):
        series = 1.0 - twice * (1.0 / order) * series
    return resid * jnp.sqrt(jnp.where(twice < 0.25, twice * series, 1.0 - jnp.exp(-twice)))


def local_kernel(part, tail, height, halo_ref, q_ref, taps_ref, resid_ref, rate_ref, x_ref, start_ref, weight_ref, y_ref, qf_ref, gain_ref, piece_ref, q_rows, tap_rows, sem):
    tokens, channels = q_ref.shape
    modes = resid_ref.shape[0]
    taps = tail + 1
    parts = channels // (height * LANES)
    rows = piece_ref.shape[0]
    begin = weight_ref.shape[0] - (parts - part) * rows
    copy = pltpu.make_async_copy(weight_ref.at[pl.ds(begin, rows)], piece_ref, sem)
    copy.start()
    to_rows(halo_ref[...].astype(F32)[2 * tail : 3 * tail], q_rows, 0, part, height)
    spread(q_ref, q_rows, tail, part, height)
    to_rows(resid_ref[...], gain_ref, 0, part, height)
    to_rows(taps_ref[0], tap_rows, 0, part, height)
    tap = [tap_rows[at(j, height), :] for j in range(taps)]

    def gate(position, old):
        rows = old + [q_rows[at(position + tail, height), :]]
        qf_ref[at(position, height), :] = convolved(tap, rows)
        return rows[1:]

    lax.fori_loop(0, tokens, gate, [q_rows[at(j, height), :] for j in range(tail)], unroll=8)
    rates = [rate_ref[at(part * modes + m, height), :] for m in range(modes)]
    gain = [gain_of(rate, gain_ref[at(m, height), :]) for m, rate in enumerate(rates)]
    for m in range(modes):
        gain_ref[at(m, height), :] = gain[m]
    decay = [jnp.exp(-rate) for rate in rates]

    def step(position, state, product):
        state = [d * s + product for d, s in zip(decay, state)]
        y_ref[at(position, height), :] = summed(c * s for c, s in zip(gain, state))
        return state

    state = [jnp.zeros((height, LANES), F32)] * modes
    for position in range(tail):
        state = step(position, state, start_ref[at(part * tail + position, height), :])
    body = lambda position, state: step(position, state, x_ref[at(part * tokens + position, height), :])
    lax.fori_loop(tail, tokens, body, state, unroll=factor(tokens - tail, 8))
    copy.wait()


def weight_of(tokens, rate_ref, devices):
    return jnp.exp(-rate_ref[...] * (tokens * devices).astype(F32))


def before_of(tokens, stride, radix, rate_ref, before_ref, others):
    index = lax.axis_index("ctx")
    digit, inside = (index // stride) % radix, index % stride
    terms = [before_ref[...]]
    for j, ref in enumerate(others, 1):
        place = digit ^ j
        steps = jnp.maximum(stride * (digit - 1 - place), 0) + inside
        scale = jnp.where(place < digit, 1.0, 0.0)
        terms.append(weight_of(tokens, rate_ref, steps) * (scale * ref[...].astype(F32)))
    return summed(terms)


def join_kernel(tokens, stride, radix, rate_ref, total_ref, before_ref, *refs):
    others, (joined_ref, sent_ref, next_ref) = refs[:-3], refs[-3:]
    next_ref[...] = before_of(tokens, stride, radix, rate_ref, before_ref, others)
    digit = (lax.axis_index("ctx") // stride) % radix
    terms = [weight_of(tokens, rate_ref, stride * (radix - 1 - digit)) * total_ref[...]]
    for j, ref in enumerate(others, 1):
        terms.append(weight_of(tokens, rate_ref, stride * (radix - 1 - (digit ^ j))) * ref[...].astype(F32))
    joined_ref[...] = summed(terms)
    sent_ref[...] = joined_ref[...].astype(BF16)


def carry_kernel(height, stride, radix, rate_ref, before_ref, *refs):
    gated_ref, carry_ref, rows = refs[-3:]
    tokens = gated_ref.shape[0]
    others, refs = refs[: radix - 1], refs[radix - 1 : -3]
    carry_ref[...] = before_of(tokens, stride, radix, rate_ref, before_ref, others)
    parts = len(refs) // 3
    modes = rate_ref.shape[0] // (height * parts)
    for part in range(parts):
        y_ref, qf_ref, gain_ref = refs[3 * part : 3 * part + 3]
        decay = [jnp.exp(-rate_ref[at(part * modes + m, height), :]) for m in range(modes)]
        start = [gain_ref[at(m, height), :] * carry_ref[at(part * modes + m, height), :] for m in range(modes)]

        def body(position, state, decay=decay, y_ref=y_ref, qf_ref=qf_ref):
            here_ = at(position, height)
            state = [d * s for d, s in zip(decay, state)]
            rows[here_, :] = qf_ref[here_, :] * rounded(y_ref[here_, :] + summed(state))
            return state

        lax.fori_loop(0, tokens, body, start, unroll=8)
        step = 16

        def gather(index, carry, part=part):
            begin = pl.multiple_of(index * step, step)
            for group in range(height):
                lane = (part * height + group) * LANES
                piece = rows[pl.ds(begin * height + group, step, stride=height), :]
                gated_ref[pl.ds(begin, step), lane : lane + LANES] = piece.astype(BF16)
            return carry

        lax.fori_loop(0, tokens // step, gather, 0)


def matmul_kernel(bits, gated_ref, *refs):
    out_ref = refs[-1]
    columns = out_ref.shape[1]
    block = pl.ds(pl.multiple_of((lax.axis_index("tp") ^ bits) * columns, LANES), columns)
    first, total = 0, None
    for piece_ref in refs[:-1]:
        rows = piece_ref.shape[0]
        term = jnp.dot(gated_ref[:, first : first + rows], piece_ref[:, block], preferred_element_type=F32)
        total = term if total is None else total + term
        first += rows
    out_ref[...] = total.astype(out_ref.dtype)


def project(gated, pieces, bits, columns, kind):
    tokens, channels = gated.shape
    return pl.pallas_call(
        functools.partial(matmul_kernel, bits),
        in_specs=[here()] * (1 + len(pieces)),
        out_specs=here(),
        out_shape=jax.ShapeDtypeStruct((tokens, columns), kind),
        compiler_params=SMALL,
        cost_estimate=pl.CostEstimate(
            flops=2 * tokens * channels * columns,
            bytes_accessed=2 * channels * columns,
            transcendentals=0,
        ),
    )(gated, *pieces)


def swap(value, axis, bits):
    count = lax.axis_size(axis)
    return lax.ppermute(value, axis, [(i, i ^ bits) for i in range(count)])


def radices(count):
    found = []
    while count > 1:
        found.append(2 if not found or count == 2 else 4)
        count //= found[-1]
    return found


def exchange(sent, stride, radix):
    far_first = {j: swap(sent, "ctx", j * stride) for j in reversed(range(1, radix))}
    return [far_first[j] for j in range(1, radix)]


def shards(queries, keys, values, short_taps, long_rates, long_resid, out_weight):
    tokens, channels = queries.shape
    taps = short_taps.shape[1]
    modes = long_rates.shape[1]
    tail = taps - 1
    height = min(SUBLANES, channels // LANES)
    parts = channels // (height * LANES)
    shape = jax.ShapeDtypeStruct
    rows = lambda count, kind=F32: shape((count * height, LANES), kind)
    scratch = lambda count: VMEM((count * height, LANES), F32)

    out_weight = pltpu.with_memory_space_constraint(out_weight, pltpu.HBM)
    arguments = (keys, values, queries, short_taps, long_rates.T, long_resid.T)
    ends, keys, values, queries, short_taps, rates, resid = pl.pallas_call(
        functools.partial(fetch_kernel, tail),
        in_specs=[far()] * len(arguments),
        out_specs=[here()] * (1 + len(arguments)),
        out_shape=[shape((3 * tail, channels), BF16)] + [shape(a.shape, a.dtype) for a in arguments],
        scratch_shapes=[pltpu.SemaphoreType.DMA((len(arguments),))],
        compiler_params=SMALL,
    )(*[pltpu.with_memory_space_constraint(a, pltpu.HBM) for a in arguments])
    count = lax.axis_size("ctx")
    halo = lax.ppermute(ends, "ctx", [(i, i + 1) for i in range(count - 1)])

    product, part_state, rate, tap, piece = pl.pallas_call(
        functools.partial(state_kernel, tail, height),
        in_specs=[here()] * 4 + [far()],
        out_specs=[here()] * 5,
        out_shape=[
            rows(parts * tokens),
            rows(parts * modes),
            rows(parts * modes),
            rows(parts * 2 * taps),
            shape((channels // 2, out_weight.shape[1]), BF16),
        ],
        scratch_shapes=[scratch(tokens), scratch(tokens), pltpu.SemaphoreType.DMA],
        compiler_params=SMALL,
        cost_estimate=pl.CostEstimate(flops=2 * tokens * channels * modes, bytes_accessed=channels * out_weight.shape[1], transcendentals=0),
    )(keys, values, short_taps, rates, out_weight)
    pieces = [piece]

    start, total, sent = pl.pallas_call(
        functools.partial(first_kernel, tail, height),
        in_specs=[here()] * 6,
        out_specs=[here()] * 3,
        out_shape=[rows(parts * tail), rows(parts * modes), rows(parts * modes, BF16)],
        scratch_shapes=[scratch(tail + taps), scratch(tail + taps)],
        compiler_params=SMALL,
    )(halo, keys, values, tap, rate, part_state)

    local = []
    for part in range(parts):
        *found, piece = pl.pallas_call(
            functools.partial(local_kernel, part, tail, height),
            in_specs=[here()] * 7 + [far()],
            out_specs=[here()] * 4,
            out_shape=[
                rows(tokens),
                rows(tokens),
                rows(modes),
                shape((channels // (2 * parts), out_weight.shape[1]), BF16),
            ],
            scratch_shapes=[scratch(tokens + tail), scratch(taps), pltpu.SemaphoreType.DMA],
            compiler_params=SMALL,
            cost_estimate=pl.CostEstimate(
                flops=4 * tokens * channels * modes // parts, bytes_accessed=channels * out_weight.shape[1] // parts, transcendentals=0
            ),
        )(halo, queries, short_taps, resid, rate, product, start, out_weight)
        local += found
        pieces.append(piece)

    before = jnp.zeros((parts * modes * height, LANES), F32)
    stride = 1
    steps = radices(count) or [1]
    for radix in steps[:-1]:
        others = exchange(sent, stride, radix)
        total, sent, before = pl.pallas_call(
            functools.partial(join_kernel, tokens, stride, radix),
            in_specs=[here()] * (3 + len(others)),
            out_specs=[here()] * 3,
            out_shape=[rows(parts * modes), rows(parts * modes, BF16), rows(parts * modes)],
            compiler_params=SMALL,
        )(rate, total, before, *others)
        stride *= radix
    others = exchange(sent, stride, steps[-1])
    gated = pl.pallas_call(
        functools.partial(carry_kernel, height, stride, steps[-1]),
        in_specs=[here()] * (2 + len(others) + len(local)),
        out_specs=here(),
        out_shape=shape((tokens, channels), BF16),
        scratch_shapes=[scratch(parts * modes), scratch(tokens)],
        compiler_params=SMALL,
    )(rate, before, *others, *local)

    ranks = lax.axis_size("tp")
    columns = out_weight.shape[1] // ranks
    cores = 2 if ranks % 2 == 0 else 1
    arrived = []
    own = None
    for chip in reversed(range(0, ranks, cores)):
        block = functools.partial(project, gated, pieces, columns=columns)
        if cores == 2:
            given = swap(block(bits=chip + 1, kind=BF16), "tp", 1)
            total = block(bits=chip, kind=F32) + given.astype(F32)
        else:
            total = block(bits=chip, kind=F32)
        if chip:
            arrived.append(swap(total.astype(BF16), "tp", chip))
        else:
            own = total
    for item in arrived:
        own = own + item.astype(F32)
    return own.astype(BF16)


def solution(mesh):
    return jax.shard_map(
        shards,
        mesh=mesh,
        in_specs=(
            P("ctx", "tp"),
            P("ctx", "tp"),
            P("ctx", "tp"),
            P(None, None, "tp"),
            P("tp", None),
            P("tp", None),
            P("tp", None),
        ),
        out_specs=P("ctx", "tp"),
        check_vma=False,
    )
```
